32 devices in a mesh: aux: 4 (over z), pair: 8 (over y, x, core).
Axes of the slice: x: 2, y: 2, z: 4, core: 2. Of those that a mesh axis runs over, the one named last changes fastest.
Arguments:
- metric: bfloat16 [4096, 4096], P('aux', 'pair'), may hold values from -0.09375 to 0.09375
- amplitudes: bfloat16 [4096, 16384], P('aux', 'pair'), may hold values from -0.59765625 to 0.59765625
- virt_coef: bfloat16 [1024, 1280], replicated, may hold values from -1.5 to 1.5
Outputs:
- density: float32 [4096, 4096], P('aux', 'pair')
- fitted_ao: bfloat16 [4096, 20480], P(('aux', 'pair'))
The draws below stay inside these ranges and needn't reach their ends.
All inputs are finite; a program needn't handle non-finite values.
Results may differ from the reference program's by a relative error of at most 0.012.
Values may be sent and summed in bfloat16 or wider, within the bound.
A program may use at most 128 MiB of HBM per device.

```python
import jax
import jax.numpy as jnp
from jax import lax

P_SIZE = 4096
V = 1024
AO = 1280
OCC = 16
PAIRS = 16384


def raised(drawn, key, source, target, blocks, factor):
    owner, partner = [(jnp.arange(drawn.shape[position]) // (drawn.shape[position] // blocks)).reshape([-1 if axis == position else 1 for axis in range(drawn.ndim)]) for position in (source, target)]
    chosen = jax.random.permutation(key, blocks)[partner]
    strong = (owner == chosen) | (owner == (partner + blocks // 2) % blocks)
    return jnp.where(strong, factor * drawn, drawn)


def block_levels(key, shape, cuts, least, top_value):
    factor_of, own = 1.0, jax.random.fold_in(key, 6)
    for axis_at, parts in cuts:
        heights = jnp.exp(jax.random.uniform(jax.random.fold_in(own, axis_at), (parts,), jnp.float32, least / len(cuts), top_value / len(cuts)))
        factor_of = factor_of * jnp.repeat(heights, shape[axis_at] // parts).reshape([-1 if axis == axis_at else 1 for axis in range(len(shape))])
    return factor_of


def bell_draw(own_key, dims, deviation, limit, cuts=(), dtype=jnp.bfloat16):
    gain = block_levels(own_key, dims, cuts, -0.22, 0.18) if cuts else 1.0
    array = jax.random.normal(own_key, dims, jnp.float32) * deviation * gain
    return jnp.minimum(jnp.maximum(array, -limit), limit).astype(dtype)


def heavy_noise(stream_key, shape, width, reach, pieces, heavy, kind=jnp.bfloat16):
    entries = width * jax.random.normal(stream_key, shape, jnp.float32)
    if pieces:
        entries = entries * block_levels(stream_key, shape, pieces, -0.22, 0.18)
    return jnp.clip(raised(entries, jax.random.fold_in(stream_key, 3), *heavy), -reach, reach).astype(kind)


def setup_inputs(seed: int = 0) -> dict:
    streams_of = jax.random.split(jax.random.key(seed), 4)
    return {
        "metric": bell_draw(streams_of[0], (P_SIZE, P_SIZE), P_SIZE ** -0.5, 0.09375, ((0, 4), (1, 8))),
        "amplitudes": heavy_noise(streams_of[1], (P_SIZE, PAIRS), 0.1, 0.59765625, ((0, 4), (1, 8)), (1, 0, 8, 2.0)),
        "virt_coef": bell_draw(streams_of[2], (V, AO), (V // 64) ** -0.5, 1.5),
    }


def reference(metric, amplitudes, virt_coef):
    fitted = jnp.dot(metric, amplitudes, preferred_element_type=jnp.float32).astype(jnp.bfloat16)
    density = lax.dot_general(fitted, amplitudes, (((1,), (1,)), ((), ())), preferred_element_type=jnp.float32)
    blocks = fitted.reshape(P_SIZE * OCC, V)
    fitted_ao = jnp.dot(blocks, virt_coef, preferred_element_type=jnp.float32).astype(jnp.bfloat16)
    return density, fitted_ao.reshape(P_SIZE, OCC * AO)
```

```python
import functools

import jax
import jax.numpy as jnp
from jax import lax
from jax.experimental import pallas as pl
from jax.experimental.pallas import tpu as pltpu
from jax.sharding import PartitionSpec as P


def gather_metric(metric, n):
    me = lax.axis_index("pair")
    rows, width = metric.shape
    full = jnp.zeros((rows, n * width), metric.dtype)
    full = lax.dynamic_update_slice(full, metric, (0, me * width))
    for step in range(1, n):
        block = lax.ppermute(metric, "pair", [(i, i ^ step) for i in range(n)])
        full = lax.dynamic_update_slice(full, block, (0, (me ^ step) * width))
    return full


def ao_kernel(*refs):
    left, right, out = refs[0], refs[1], refs[-1]
    out[...] = jnp.dot(left[0], right[...], preferred_element_type=jnp.float32).astype(out.dtype)


def ao_call(blocks, virt_coef, previous, position, stride):
    sources, rows, virt = blocks.shape
    ao = virt_coef.shape[1]
    in_specs = [
        pl.BlockSpec((1, rows, virt), lambda s: (s, 0, 0)),
        pl.BlockSpec((virt, ao), lambda s: (0, 0)),
    ]
    operands = [blocks, virt_coef]
    aliases = {}
    if previous is not None:
        in_specs.append(pl.BlockSpec(memory_space=pl.ANY))
        operands.append(previous)
        aliases = {2: 0}
    return pl.pallas_call(
        ao_kernel,
        grid=(sources,),
        in_specs=in_specs,
        out_specs=pl.BlockSpec((rows, ao), lambda s: (0, s * stride + position)),
        out_shape=jax.ShapeDtypeStruct((rows, sources * stride * ao), jnp.bfloat16),
        input_output_aliases=aliases,
        cost_estimate=pl.CostEstimate(
            flops=2 * sources * rows * virt * ao,
            bytes_accessed=2 * (sources * rows * (virt + ao) + virt * ao),
            transcendentals=0,
        ),
    )(*operands)


def density_part(fitted, amp, parity, n, earlier):
    width = amp.shape[0] // n
    rows = amp.reshape(n // 2, 2, width, amp.shape[1])
    rows = lax.dynamic_index_in_dim(rows, parity, axis=1, keepdims=False)
    rows = rows.reshape(n // 2 * width, amp.shape[1])
    value = lax.dot_general(fitted, rows, (((1,), (1,)), ((), ())), preferred_element_type=jnp.float32)
    return value if earlier is None else earlier + value


def shards(n, metric, amplitudes, virt_coef):
    parity = lax.axis_index("pair") % 2
    per = amplitudes.shape[1]
    virt = virt_coef.shape[0]
    ao = virt_coef.shape[1]
    count = 4 if per % (4 * 128) == 0 else 1
    chunk = per // count
    pieces = [amplitudes[:, c * chunk : (c + 1) * chunk] for c in range(count)]
    gathered = [lax.all_gather(piece, "aux", axis=0, tiled=True) for piece in pieces]
    rows_metric = gather_metric(metric, n)
    by_occ = per % virt == 0 and (virt % chunk == 0)
    own, other, moved, fitted_ao = None, None, [], None
    for c in range(count):
        amp = gathered[c]
        fitted = jnp.dot(rows_metric, amp, preferred_element_type=jnp.float32).astype(jnp.bfloat16)
        other = density_part(fitted, amp, 1 - parity, n, other)
        own = density_part(fitted, amp, parity, n, own)
        blocks = fitted.reshape(n, fitted.shape[0] // n, chunk)
        moved.append(lax.all_to_all(blocks, "pair", split_axis=0, concat_axis=0, tiled=True))
        if by_occ and (c + 1) * chunk % virt == 0:
            group = moved[0] if len(moved) == 1 else jnp.concatenate(moved, axis=2)
            fitted_ao = ao_call(group, virt_coef, fitted_ao, (c + 1) * chunk // virt - 1, per // virt)
            moved = []
    arrived = lax.ppermute(other.astype(jnp.bfloat16), "pair", [(i, i ^ 1) for i in range(n)])
    summed = (own + arrived.astype(jnp.float32)).astype(jnp.bfloat16)
    groups = [[i for i in range(n) if i % 2 == q] for q in range(2)]
    density = lax.psum_scatter(
        summed, "pair", scatter_dimension=1, axis_index_groups=groups, tiled=True
    ).astype(jnp.float32)
    if not by_occ:
        whole = jnp.concatenate(moved, axis=2)
        whole = whole.transpose(1, 0, 2).reshape(-1, virt)
        fitted_ao = jnp.dot(whole, virt_coef, preferred_element_type=jnp.float32).astype(jnp.bfloat16)
        fitted_ao = fitted_ao.reshape(amplitudes.shape[0] // n, -1)
    return density, fitted_ao


def solution(mesh):
    in_specs = (P("aux", "pair"), P("aux", "pair"), P())
    out_specs = (P("aux", "pair"), P(("aux", "pair"), None))
    body = functools.partial(shards, mesh.shape["pair"])
    return jax.shard_map(body, mesh=mesh, in_specs=in_specs, out_specs=out_specs, check_vma=False)
```

```python
import functools

import jax
import jax.numpy as jnp
from jax import lax
from jax.experimental import pallas as pl
from jax.experimental.pallas import tpu as pltpu
from jax.sharding import PartitionSpec as P

MESH = pl.DeviceIdType.MESH


def kernel(
    na, n, count, metric, amp, virt_coef, density, fitted_ao,
    m_v, a_v, d_v, f_v, g_v, c_v, one_v, two_v, o_v,
    m_send, m_recv, z_send, z_recv, x_send, x_recv, one_send, one_recv, two_send, two_recv, o_sem, local_sem,
):
    a, b = lax.axis_index("aux"), lax.axis_index("pair")
    p, q = metric.shape
    per = amp.shape[1]
    w = per // count
    rows = p // n
    virt, ao = virt_coef.shape
    half = n // 2
    parity, chip = lax.rem(b, 2), b // 2
    partner = b + 1 - 2 * parity
    tile = min(256, p)
    tiles = p // tile

    barrier = pltpu.get_barrier_semaphore()
    for d in range(1, n):
        pl.semaphore_signal(barrier, inc=1, device_id=(a, lax.rem(b + d, n)), device_id_type=MESH)

    @pl.when(a > 0)
    def _():
        pl.semaphore_signal(barrier, inc=1, device_id=(a - 1, b), device_id_type=MESH)

    @pl.when(a < na - 1)
    def _():
        pl.semaphore_signal(barrier, inc=1, device_id=(a + 1, b), device_id_type=MESH)

    pl.semaphore_wait(barrier, n - 1 + jnp.where(a > 0, 1, 0) + jnp.where(a < na - 1, 1, 0))

    def block_of(s, c):
        return a_v.at[c, pl.ds(pl.multiple_of(s * p, p), p), :]

    def hop(src, s, c, way, target):
        return pltpu.make_async_remote_copy(
            src_ref=src, dst_ref=block_of(s, c), send_sem=z_send.at[way, s, c],
            recv_sem=z_recv.at[s, c], device_id=(target, b), device_id_type=MESH,
        )

    def metric_copy(owner, target):
        return pltpu.make_async_remote_copy(
            src_ref=metric, dst_ref=m_v.at[:, pl.ds(pl.multiple_of(owner * q, q), q)],
            send_sem=m_send.at[target], recv_sem=m_recv.at[owner],
            device_id=(a, target), device_id_type=MESH,
        )

    def regroup(owner, target, c):
        return pltpu.make_async_remote_copy(
            src_ref=f_v.at[c, pl.ds(pl.multiple_of(target * rows, rows), rows), :],
            dst_ref=g_v.at[:, pl.ds(pl.multiple_of(owner * per + c * w, w), w)],
            send_sem=x_send.at[target, c], recv_sem=x_recv.at[owner, c],
            device_id=(a, target), device_id_type=MESH,
        )

    def staged(j):
        return m_v.at[:, pl.ds(pl.multiple_of(j * q, q), q)]

    def first(j):
        return pltpu.make_async_remote_copy(
            src_ref=staged(j), dst_ref=one_v.at[j // 2], send_sem=one_send.at[j // 2],
            recv_sem=one_recv.at[j // 2], device_id=(a, partner), device_id_type=MESH,
        )

    def second(source, j):
        return pltpu.make_async_remote_copy(
            src_ref=staged(j), dst_ref=two_v.at[source], send_sem=two_send.at[j // 2],
            recv_sem=two_recv.at[source], device_id=(a, j), device_id_type=MESH,
        )

    def mine(c):
        return amp.at[:, c * w : (c + 1) * w]

    for c in range(count):
        @pl.when(a > 0)
        def _():
            hop(mine(c), a, c, 0, jnp.maximum(a - 1, 0)).start()

        @pl.when(a < na - 1)
        def _():
            hop(mine(c), a, c, 1, jnp.minimum(a + 1, na - 1)).start()

    @pl.loop(1, n)
    def _(d):
        metric_copy(b, lax.rem(b + d, n)).start()

    own_copies = [pltpu.make_async_copy(mine(c), block_of(a, c), local_sem.at[c]) for c in range(count)]
    own_copies.append(pltpu.make_async_copy(metric, staged(b), local_sem.at[count]))
    own_copies.append(pltpu.make_async_copy(virt_coef, c_v, local_sem.at[count + 1]))
    for copy in own_copies:
        copy.start()

    def arrive(t, c):
        @pl.when(a - t >= 0)
        def _():
            s = jnp.maximum(a - t, 0)
            hop(block_of(s, c), s, c, 1, a).wait_recv()

            @pl.when(a < na - 1)
            def _():
                hop(block_of(s, c), s, c, 1, jnp.minimum(a + 1, na - 1)).start()

        @pl.when(a + t < na)
        def _():
            s = jnp.minimum(a + t, na - 1)
            hop(block_of(s, c), s, c, 0, a).wait_recv()

            @pl.when(a > 0)
            def _():
                hop(block_of(s, c), s, c, 0, jnp.maximum(a - 1, 0)).start()

    @pl.loop(1, na - 1)
    def _(t):
        @pl.loop(0, count)
        def _(c):
            arrive(t, c)

    for copy in own_copies:
        copy.wait()

    @pl.loop(1, n)
    def _(d):
        metric_copy(lax.rem(b + n - d, n), b).wait_recv()

    @pl.loop(1, n)
    def _(d):
        metric_copy(b, lax.rem(b + d, n)).wait_send()

    def row(r):
        return pl.ds(pl.multiple_of(r * tile, tile), tile)

    def product(j, r, c):
        right = a_v[c, pl.ds(pl.multiple_of(j * q, q), q), :]
        return lax.dot_general(
            f_v[c, row(r), :], right, (((1,), (1,)), ((), ())), preferred_element_type=jnp.float32
        )

    def fit(c):
        @pl.loop(0, tiles)
        def _(r):
            f_v[c, row(r), :] = jnp.dot(
                m_v[row(r), :], a_v[c], preferred_element_type=jnp.float32
            ).astype(f_v.dtype)

        @pl.loop(1, n)
        def _(d):
            regroup(b, lax.rem(b + d, n), c).start()

        pltpu.make_async_copy(
            f_v.at[c, pl.ds(pl.multiple_of(b * rows, rows), rows), :],
            g_v.at[:, pl.ds(pl.multiple_of(b * per + c * w, w), w)], x_send.at[b, c],
        ).start()

    @pl.loop(0, n * tiles)
    def _(i):
        d_v[i // tiles, row(lax.rem(i, tiles)), :] = jnp.zeros((tile, q), jnp.float32)

    @pl.loop(0, count - 1)
    def _(c):
        arrive(na - 1, c)
        fit(c)

        @pl.loop(0, n * tiles)
        def _(i):
            j, r = i // tiles, lax.rem(i, tiles)
            d_v[j, row(r), :] += product(j, r, c)

    last = count - 1
    arrive(na - 1, last)
    fit(last)

    @pl.loop(0, half)
    def _(h):
        j = 2 * lax.rem(chip + h, half) + 1 - parity

        @pl.loop(0, tiles)
        def _(r):
            m_v[row(r), pl.ds(pl.multiple_of(j * q, q), q)] = (
                d_v[j, row(r), :] + product(j, r, last)
            ).astype(m_v.dtype)

        first(j).start()

    @pl.loop(0, half)
    def _(h):
        j = 2 * lax.rem(chip + h, half) + parity

        @pl.loop(0, tiles)
        def _(r):
            d_v[j, row(r), :] += product(j, r, last)

    @pl.loop(1, half)
    def _(h):
        slot = lax.rem(chip + h, half)
        j = 2 * slot + parity
        first(j).wait_recv()

        @pl.loop(0, tiles)
        def _(r):
            m_v[row(r), pl.ds(pl.multiple_of(j * q, q), q)] = (
                d_v[j, row(r), :] + one_v[slot, row(r), :].astype(jnp.float32)
            ).astype(m_v.dtype)

        second(chip, j).start()

    first(b).wait_recv()

    @pl.loop(0, tiles)
    def _(r):
        d_v[b, row(r), :] += one_v[chip, row(r), :].astype(jnp.float32)

    @pl.loop(0, count)
    def _(c):
        pltpu.make_async_copy(
            f_v.at[c, pl.ds(pl.multiple_of(b * rows, rows), rows), :],
            g_v.at[:, pl.ds(pl.multiple_of(b * per + c * w, w), w)], x_send.at[b, c],
        ).wait()

        @pl.loop(1, n)
        def _(d):
            regroup(lax.rem(b + n - d, n), b, c).wait_recv()

    occ = n * per // virt

    def out_copy(i, slot):
        return pltpu.make_async_copy(
            o_v.at[slot], fitted_ao.at[:, pl.ds(pl.multiple_of(i * ao, ao), ao)], o_sem.at[slot]
        )

    @pl.loop(0, occ)
    def _(i):
        slot = lax.rem(i, 2)

        @pl.when(i >= 2)
        def _():
            out_copy(i - 2, slot).wait()

        o_v[slot] = jnp.dot(
            g_v[:, pl.ds(pl.multiple_of(i * virt, virt), virt)], c_v[...], preferred_element_type=jnp.float32
        ).astype(o_v.dtype)
        out_copy(i, slot).start()

    for i in range(max(occ - 2, 0), occ):
        out_copy(i, i % 2).wait()

    @pl.loop(1, half)
    def _(h):
        source = lax.rem(chip + half - h, half)
        second(source, b).wait_recv()

        @pl.loop(0, tiles)
        def _(r):
            d_v[b, row(r), :] += two_v[source, row(r), :].astype(jnp.float32)

    result = pltpu.make_async_copy(d_v.at[b], density, local_sem.at[0])
    result.start()

    @pl.loop(0, half)
    def _(h):
        first(2 * h + 1 - parity).wait_send()

    @pl.loop(1, half)
    def _(h):
        second(chip, 2 * lax.rem(chip + h, half) + parity).wait_send()

    @pl.loop(0, count)
    def _(c):
        @pl.loop(1, n)
        def _(d):
            regroup(b, lax.rem(b + d, n), c).wait_send()

        @pl.loop(0, na)
        def _(s):
            @pl.when(jnp.logical_and(s >= a, a > 0))
            def _():
                hop(block_of(s, c), s, c, 0, jnp.maximum(a - 1, 0)).wait_send()

            @pl.when(jnp.logical_and(s <= a, a < na - 1))
            def _():
                hop(block_of(s, c), s, c, 1, jnp.minimum(a + 1, na - 1)).wait_send()

    result.wait()


def shards(na, n, metric, amplitudes, virt_coef):
    p, q = metric.shape
    per = amplitudes.shape[1]
    virt, ao = virt_coef.shape
    count = 4
    w = per // count
    rows = p // n
    bf16 = jnp.bfloat16
    dma = pltpu.SemaphoreType.DMA
    return pl.pallas_call(
        functools.partial(kernel, na, n, count),
        out_shape=(
            jax.ShapeDtypeStruct((p, q), jnp.float32),
            jax.ShapeDtypeStruct((rows, n * per // virt * ao), bf16),
        ),
        in_specs=[pl.BlockSpec(memory_space=pl.ANY)] * 3,
        out_specs=(pl.BlockSpec(memory_space=pl.ANY), pl.BlockSpec(memory_space=pl.ANY)),
        scratch_shapes=[
            pltpu.VMEM((p, n * q), bf16),
            pltpu.VMEM((count, na * p, w), bf16),
            pltpu.VMEM((n, p, q), jnp.float32),
            pltpu.VMEM((count, p, w), bf16),
            pltpu.VMEM((rows, n * per), bf16),
            pltpu.VMEM((virt, ao), bf16),
            pltpu.VMEM((n // 2, p, q), bf16),
            pltpu.VMEM((n // 2, p, q), bf16),
            pltpu.VMEM((2, rows, ao), bf16),
            dma((n,)), dma((n,)),
            dma((2, na, count)), dma((na, count)),
            dma((n, count)), dma((n, count)),
            dma((n // 2,)), dma((n // 2,)),
            dma((n // 2,)), dma((n // 2,)),
            dma((2,)), dma((count + 2,)),
        ],
        compiler_params=pltpu.CompilerParams(
            collective_id=0, has_side_effects=True, vmem_limit_bytes=67043328
        ),
    )(metric, amplitudes, virt_coef)


def solution(mesh):
    in_specs = (P("aux", "pair"), P("aux", "pair"), P())
    out_specs = (P("aux", "pair"), P(("aux", "pair"), None))
    body = functools.partial(shards, mesh.shape["aux"], mesh.shape["pair"])
    return jax.shard_map(body, mesh=mesh, in_specs=in_specs, out_specs=out_specs, check_vma=False)
```

```python
import functools

import jax
import jax.numpy as jnp
from jax import lax
from jax.experimental import pallas as pl
from jax.experimental.pallas import tpu as pltpu
from jax.sharding import PartitionSpec as P

MESH = pl.DeviceIdType.MESH


def kernel(
    na, n, count, metric, amp, virt_coef, density, fitted_ao,
    m_v, a_v, d_v, f_v, g_v, c_v, one_v, two_v, o_v,
    m_send, m_recv, z_send, z_recv, x_send, x_recv, one_send, one_recv, two_send, two_recv, o_sem, local_sem,
):
    a, b = lax.axis_index("aux"), lax.axis_index("pair")
    p, q = metric.shape
    per = amp.shape[1]
    w = per // count
    rows = p // n
    virt, ao = virt_coef.shape
    half = n // 2
    parity, chip = lax.rem(b, 2), b // 2
    partner = b + 1 - 2 * parity
    tile = min(256, p)
    tiles = p // tile

    barrier = pltpu.get_barrier_semaphore()
    for d in range(1, n):
        pl.semaphore_signal(barrier, inc=1, device_id=(a, lax.rem(b + d, n)), device_id_type=MESH)

    @pl.when(a > 0)
    def _():
        pl.semaphore_signal(barrier, inc=1, device_id=(a - 1, b), device_id_type=MESH)

    @pl.when(a < na - 1)
    def _():
        pl.semaphore_signal(barrier, inc=1, device_id=(a + 1, b), device_id_type=MESH)

    pl.semaphore_wait(barrier, n - 1 + jnp.where(a > 0, 1, 0) + jnp.where(a < na - 1, 1, 0))

    def block_of(s, c):
        return a_v.at[c, pl.ds(pl.multiple_of(s * p, p), p), :]

    def hop(src, s, c, way, target):
        return pltpu.make_async_remote_copy(
            src_ref=src, dst_ref=block_of(s, c), send_sem=z_send.at[way, s, c],
            recv_sem=z_recv.at[s, c], device_id=(target, b), device_id_type=MESH,
        )

    def metric_copy(owner, target):
        return pltpu.make_async_remote_copy(
            src_ref=metric, dst_ref=m_v.at[:, pl.ds(pl.multiple_of(owner * q, q), q)],
            send_sem=m_send.at[target], recv_sem=m_recv.at[owner],
            device_id=(a, target), device_id_type=MESH,
        )

    def regroup(owner, target, c):
        return pltpu.make_async_remote_copy(
            src_ref=f_v.at[c, pl.ds(pl.multiple_of(target * rows, rows), rows), :],
            dst_ref=g_v.at[:, pl.ds(pl.multiple_of(owner * per + c * w, w), w)],
            send_sem=x_send.at[target, c], recv_sem=x_recv.at[owner, c],
            device_id=(a, target), device_id_type=MESH,
        )

    def staged(j):
        return m_v.at[:, pl.ds(pl.multiple_of(j * q, q), q)]

    def first(j):
        return pltpu.make_async_remote_copy(
            src_ref=staged(j), dst_ref=one_v.at[j // 2], send_sem=one_send.at[j // 2],
            recv_sem=one_recv.at[j // 2], device_id=(a, partner), device_id_type=MESH,
        )

    def second(source, j):
        return pltpu.make_async_remote_copy(
            src_ref=staged(j), dst_ref=two_v.at[source], send_sem=two_send.at[0, j // 2],
            recv_sem=two_recv.at[0, source], device_id=(a, j), device_id_type=MESH,
        )

    def mine(c):
        return amp.at[:, c * w : (c + 1) * w]

    for c in range(count):
        @pl.when(a > 0)
        def _():
            hop(mine(c), a, c, 0, jnp.maximum(a - 1, 0)).start()

        @pl.when(a < na - 1)
        def _():
            hop(mine(c), a, c, 1, jnp.minimum(a + 1, na - 1)).start()

    @pl.loop(1, n)
    def _(d):
        metric_copy(b, lax.rem(b + d, n)).start()

    own_copies = [pltpu.make_async_copy(mine(c), block_of(a, c), local_sem.at[c]) for c in range(count)]
    own_copies.append(pltpu.make_async_copy(metric, staged(b), local_sem.at[count]))
    own_copies.append(pltpu.make_async_copy(virt_coef, c_v, local_sem.at[count + 1]))
    for copy in own_copies:
        copy.start()

    def arrive(t, c):
        @pl.when(a - t >= 0)
        def _():
            s = jnp.maximum(a - t, 0)
            hop(block_of(s, c), s, c, 1, a).wait_recv()

            @pl.when(a < na - 1)
            def _():
                hop(block_of(s, c), s, c, 1, jnp.minimum(a + 1, na - 1)).start()

        @pl.when(a + t < na)
        def _():
            s = jnp.minimum(a + t, na - 1)
            hop(block_of(s, c), s, c, 0, a).wait_recv()

            @pl.when(a > 0)
            def _():
                hop(block_of(s, c), s, c, 0, jnp.maximum(a - 1, 0)).start()

    @pl.loop(1, na - 1)
    def _(t):
        @pl.loop(0, count)
        def _(c):
            arrive(t, c)

    for copy in own_copies:
        copy.wait()

    @pl.loop(1, n)
    def _(d):
        metric_copy(lax.rem(b + n - d, n), b).wait_recv()

    @pl.loop(1, n)
    def _(d):
        metric_copy(b, lax.rem(b + d, n)).wait_send()

    def row(r):
        return pl.ds(pl.multiple_of(r * tile, tile), tile)

    def product(j, r, c):
        right = a_v[c, pl.ds(pl.multiple_of(j * q, q), q), :]
        return lax.dot_general(
            f_v[c, row(r), :], right, (((1,), (1,)), ((), ())), preferred_element_type=jnp.float32
        )

    def fit(c):
        @pl.loop(0, tiles)
        def _(r):
            f_v[c, row(r), :] = jnp.dot(
                m_v[row(r), :], a_v[c], preferred_element_type=jnp.float32
            ).astype(f_v.dtype)

        @pl.loop(1, n)
        def _(d):
            regroup(b, lax.rem(b + d, n), c).start()

        pltpu.make_async_copy(
            f_v.at[c, pl.ds(pl.multiple_of(b * rows, rows), rows), :],
            g_v.at[:, pl.ds(pl.multiple_of(b * per + c * w, w), w)], x_send.at[b, c],
        ).start()

    @pl.loop(0, n * tiles)
    def _(i):
        d_v[i // tiles, row(lax.rem(i, tiles)), :] = jnp.zeros((tile, q), jnp.float32)

    @pl.loop(0, count - 1)
    def _(c):
        arrive(na - 1, c)
        fit(c)

        @pl.loop(0, n * tiles)
        def _(i):
            j, r = i // tiles, lax.rem(i, tiles)
            d_v[j, row(r), :] += product(j, r, c)

    last = count - 1
    arrive(na - 1, last)
    fit(last)

    @pl.loop(0, half)
    def _(h):
        j = 2 * lax.rem(chip + h, half) + 1 - parity

        @pl.loop(0, tiles)
        def _(r):
            m_v[row(r), pl.ds(pl.multiple_of(j * q, q), q)] = (
                d_v[j, row(r), :] + product(j, r, last)
            ).astype(m_v.dtype)

        first(j).start()

    @pl.loop(0, half)
    def _(h):
        j = 2 * lax.rem(chip + h, half) + parity

        @pl.loop(0, tiles)
        def _(r):
            d_v[j, row(r), :] += product(j, r, last)

    quad = half == 4
    mid = p // 2
    near = (chip + 1 - 2 * lax.rem(chip, 2), lax.rem(chip + 2, 4))
    far = 3 - chip

    def part(way):
        return pl.ds(way * mid, mid)

    def cast(slot, way):
        j = 2 * slot + parity
        m_v[part(way), pl.ds(pl.multiple_of(j * q, q), q)] = d_v[j, part(way), :].astype(m_v.dtype)

    def piece(slot, way, place, target):
        j = 2 * slot + parity
        return pltpu.make_async_remote_copy(
            src_ref=m_v.at[part(way), pl.ds(pl.multiple_of(j * q, q), q)],
            dst_ref=two_v.at[place, part(way), :], send_sem=two_send.at[way, place],
            recv_sem=two_recv.at[way, place], device_id=(a, 2 * target + parity), device_id_type=MESH,
        )

    def add_in(slot, place, way):
        j = 2 * slot + parity
        d_v[j, part(way), :] += two_v[place, part(way), :].astype(jnp.float32)

    if quad:
        for h in range(4):
            slot = (far, near[0], near[1], chip)[h]
            first(2 * slot + parity).wait_recv()

            @pl.loop(0, tiles)
            def _(r, slot=slot):
                j = 2 * slot + parity
                d_v[j, row(r), :] += one_v[slot, row(r), :].astype(jnp.float32)

            if h == 0:
                for way in range(2):
                    cast(far, way)
                    piece(far, way, 0, near[way]).start()
            elif h < 3:
                cast(near[h - 1], h - 1)
                piece(near[h - 1], h - 1, 1, near[h - 1]).start()
    else:
        @pl.loop(1, half)
        def _(h):
            slot = lax.rem(chip + h, half)
            j = 2 * slot + parity
            first(j).wait_recv()

            @pl.loop(0, tiles)
            def _(r):
                m_v[row(r), pl.ds(pl.multiple_of(j * q, q), q)] = (
                    d_v[j, row(r), :] + one_v[slot, row(r), :].astype(jnp.float32)
                ).astype(m_v.dtype)

            second(chip, j).start()

        first(b).wait_recv()

        @pl.loop(0, tiles)
        def _(r):
            d_v[b, row(r), :] += one_v[chip, row(r), :].astype(jnp.float32)

    if quad:
        for way in range(2):
            other = near[1 - way]
            piece(other, way, 0, near[way]).wait_recv()
            add_in(other, 0, way)
            cast(other, way)
            piece(other, way, 2, other).start()

    @pl.loop(0, count)
    def _(c):
        pltpu.make_async_copy(
            f_v.at[c, pl.ds(pl.multiple_of(b * rows, rows), rows), :],
            g_v.at[:, pl.ds(pl.multiple_of(b * per + c * w, w), w)], x_send.at[b, c],
        ).wait()

        @pl.loop(1, n)
        def _(d):
            regroup(lax.rem(b + n - d, n), b, c).wait_recv()

    occ = n * per // virt

    def out_copy(i, slot):
        return pltpu.make_async_copy(
            o_v.at[slot], fitted_ao.at[:, pl.ds(pl.multiple_of(i * ao, ao), ao)], o_sem.at[slot]
        )

    @pl.loop(0, occ)
    def _(i):
        slot = lax.rem(i, 2)

        @pl.when(i >= 2)
        def _():
            out_copy(i - 2, slot).wait()

        o_v[slot] = jnp.dot(
            g_v[:, pl.ds(pl.multiple_of(i * virt, virt), virt)], c_v[...], preferred_element_type=jnp.float32
        ).astype(o_v.dtype)
        out_copy(i, slot).start()

    for i in range(max(occ - 2, 0), occ):
        out_copy(i, i % 2).wait()

    if quad:
        for way in range(2):
            piece(chip, way, 1, near[way]).wait_recv()
            add_in(chip, 1, way)
        for way in range(2):
            piece(chip, way, 2, near[1 - way]).wait_recv()
            add_in(chip, 2, way)
    else:
        @pl.loop(1, half)
        def _(h):
            source = lax.rem(chip + half - h, half)
            second(source, b).wait_recv()

            @pl.loop(0, tiles)
            def _(r):
                d_v[b, row(r), :] += two_v[source, row(r), :].astype(jnp.float32)

    result = pltpu.make_async_copy(d_v.at[b], density, local_sem.at[0])
    result.start()

    @pl.loop(0, half)
    def _(h):
        first(2 * h + 1 - parity).wait_send()

    if quad:
        for way in range(2):
            piece(far, way, 0, near[way]).wait_send()
            piece(near[way], way, 1, near[way]).wait_send()
            piece(near[1 - way], way, 2, near[1 - way]).wait_send()
    else:
        @pl.loop(1, half)
        def _(h):
            second(chip, 2 * lax.rem(chip + h, half) + parity).wait_send()

    @pl.loop(0, count)
    def _(c):
        @pl.loop(1, n)
        def _(d):
            regroup(b, lax.rem(b + d, n), c).wait_send()

        @pl.loop(0, na)
        def _(s):
            @pl.when(jnp.logical_and(s >= a, a > 0))
            def _():
                hop(block_of(s, c), s, c, 0, jnp.maximum(a - 1, 0)).wait_send()

            @pl.when(jnp.logical_and(s <= a, a < na - 1))
            def _():
                hop(block_of(s, c), s, c, 1, jnp.minimum(a + 1, na - 1)).wait_send()

    result.wait()


def shards(na, n, metric, amplitudes, virt_coef):
    p, q = metric.shape
    per = amplitudes.shape[1]
    virt, ao = virt_coef.shape
    count = next(c for c in (8, 4, 2, 1) if per % (128 * c) == 0)
    w = per // count
    rows = p // n
    bf16 = jnp.bfloat16
    dma = pltpu.SemaphoreType.DMA
    return pl.pallas_call(
        functools.partial(kernel, na, n, count),
        out_shape=(
            jax.ShapeDtypeStruct((p, q), jnp.float32),
            jax.ShapeDtypeStruct((rows, n * per // virt * ao), bf16),
        ),
        in_specs=[pl.BlockSpec(memory_space=pl.ANY)] * 3,
        out_specs=(pl.BlockSpec(memory_space=pl.ANY), pl.BlockSpec(memory_space=pl.ANY)),
        scratch_shapes=[
            pltpu.VMEM((p, n * q), bf16),
            pltpu.VMEM((count, na * p, w), bf16),
            pltpu.VMEM((n, p, q), jnp.float32),
            pltpu.VMEM((count, p, w), bf16),
            pltpu.VMEM((rows, n * per), bf16),
            pltpu.VMEM((virt, ao), bf16),
            pltpu.VMEM((n // 2, p, q), bf16),
            pltpu.VMEM((n // 2, p, q), bf16),
            pltpu.VMEM((2, rows, ao), bf16),
            dma((n,)), dma((n,)),
            dma((2, na, count)), dma((na, count)),
            dma((n, count)), dma((n, count)),
            dma((n // 2,)), dma((n // 2,)),
            dma((2, n // 2)), dma((2, n // 2)),
            dma((2,)), dma((count + 2,)),
        ],
        compiler_params=pltpu.CompilerParams(
            collective_id=0, has_side_effects=True, vmem_limit_bytes=67043328
        ),
    )(metric, amplitudes, virt_coef)


def solution(mesh):
    in_specs = (P("aux", "pair"), P("aux", "pair"), P())
    out_specs = (P("aux", "pair"), P(("aux", "pair"), None))
    body = functools.partial(shards, mesh.shape["aux"], mesh.shape["pair"])
    return jax.shard_map(body, mesh=mesh, in_specs=in_specs, out_specs=out_specs, check_vma=False)
```

```python
import functools

import jax
import jax.numpy as jnp
from jax import lax
from jax.experimental import pallas as pl
from jax.experimental.pallas import tpu as pltpu
from jax.sharding import PartitionSpec as P

MESH = pl.DeviceIdType.MESH


def kernel(
    na, n, count, metric, amp, virt_coef, density, fitted_ao,
    m_v, a_v, d_v, f_v, g_v, c_v, one_v, two_v, o_v,
    m_send, m_recv, z_send, z_recv, x_send, x_recv, one_send, one_recv, two_send, two_recv, o_sem, local_sem,
):
    a, b = lax.axis_index("aux"), lax.axis_index("pair")
    p, q = metric.shape
    per = amp.shape[1]
    w = per // count
    rows = p // n
    virt, ao = virt_coef.shape
    half = n // 2
    parity, chip = lax.rem(b, 2), b // 2
    partner = b + 1 - 2 * parity
    tile = min(256, p)
    tiles = p // tile

    barrier = pltpu.get_barrier_semaphore()
    for d in range(1, n):
        pl.semaphore_signal(barrier, inc=1, device_id=(a, lax.rem(b + d, n)), device_id_type=MESH)

    @pl.when(a > 0)
    def _():
        pl.semaphore_signal(barrier, inc=1, device_id=(a - 1, b), device_id_type=MESH)

    @pl.when(a < na - 1)
    def _():
        pl.semaphore_signal(barrier, inc=1, device_id=(a + 1, b), device_id_type=MESH)

    pl.semaphore_wait(barrier, n - 1 + jnp.where(a > 0, 1, 0) + jnp.where(a < na - 1, 1, 0))

    def block_of(s, c):
        return a_v.at[c, pl.ds(pl.multiple_of(s * p, p), p), :]

    def hop(src, s, c, way, target):
        return pltpu.make_async_remote_copy(
            src_ref=src, dst_ref=block_of(s, c), send_sem=z_send.at[way, s, c],
            recv_sem=z_recv.at[s, c], device_id=(target, b), device_id_type=MESH,
        )

    def metric_copy(owner, target):
        return pltpu.make_async_remote_copy(
            src_ref=metric, dst_ref=m_v.at[:, pl.ds(pl.multiple_of(owner * q, q), q)],
            send_sem=m_send.at[target], recv_sem=m_recv.at[owner],
            device_id=(a, target), device_id_type=MESH,
        )

    def regroup(owner, target, c):
        return pltpu.make_async_remote_copy(
            src_ref=f_v.at[c, pl.ds(pl.multiple_of(target * rows, rows), rows), :],
            dst_ref=g_v.at[:, pl.ds(pl.multiple_of(owner * per + c * w, w), w)],
            send_sem=x_send.at[target, c], recv_sem=x_recv.at[owner, c],
            device_id=(a, target), device_id_type=MESH,
        )

    def staged(j):
        return m_v.at[:, pl.ds(pl.multiple_of(j * q, q), q)]

    def first(j):
        return pltpu.make_async_remote_copy(
            src_ref=staged(j), dst_ref=one_v.at[j // 2], send_sem=one_send.at[j // 2],
            recv_sem=one_recv.at[j // 2], device_id=(a, partner), device_id_type=MESH,
        )

    def second(source, j):
        return pltpu.make_async_remote_copy(
            src_ref=staged(j), dst_ref=two_v.at[source], send_sem=two_send.at[0, j // 2],
            recv_sem=two_recv.at[0, source], device_id=(a, j), device_id_type=MESH,
        )

    def mine(c):
        return amp.at[:, c * w : (c + 1) * w]

    for c in range(count):
        @pl.when(a > 0)
        def _():
            hop(mine(c), a, c, 0, jnp.maximum(a - 1, 0)).start()

        @pl.when(a < na - 1)
        def _():
            hop(mine(c), a, c, 1, jnp.minimum(a + 1, na - 1)).start()

    @pl.loop(1, n)
    def _(d):
        metric_copy(b, lax.rem(b + d, n)).start()

    own_copies = [pltpu.make_async_copy(mine(c), block_of(a, c), local_sem.at[c]) for c in range(count)]
    own_copies.append(pltpu.make_async_copy(metric, staged(b), local_sem.at[count]))
    own_copies.append(pltpu.make_async_copy(virt_coef, c_v, local_sem.at[count + 1]))
    for copy in own_copies:
        copy.start()

    def arrive(t, c):
        @pl.when(a - t >= 0)
        def _():
            s = jnp.maximum(a - t, 0)
            hop(block_of(s, c), s, c, 1, a).wait_recv()

            @pl.when(a < na - 1)
            def _():
                hop(block_of(s, c), s, c, 1, jnp.minimum(a + 1, na - 1)).start()

        @pl.when(a + t < na)
        def _():
            s = jnp.minimum(a + t, na - 1)
            hop(block_of(s, c), s, c, 0, a).wait_recv()

            @pl.when(a > 0)
            def _():
                hop(block_of(s, c), s, c, 0, jnp.maximum(a - 1, 0)).start()

    @pl.loop(1, na - 1)
    def _(t):
        @pl.loop(0, count)
        def _(c):
            arrive(t, c)

    for copy in own_copies:
        copy.wait()

    @pl.loop(1, n)
    def _(d):
        metric_copy(lax.rem(b + n - d, n), b).wait_recv()

    @pl.loop(1, n)
    def _(d):
        metric_copy(b, lax.rem(b + d, n)).wait_send()

    def row(r):
        return pl.ds(pl.multiple_of(r * tile, tile), tile)

    def product(j, r, c):
        right = a_v[c, pl.ds(pl.multiple_of(j * q, q), q), :]
        return lax.dot_general(
            f_v[c, row(r), :], right, (((1,), (1,)), ((), ())), preferred_element_type=jnp.float32
        )

    def fit(c):
        @pl.loop(0, tiles)
        def _(r):
            f_v[c, row(r), :] = jnp.dot(
                m_v[row(r), :], a_v[c], preferred_element_type=jnp.float32
            ).astype(f_v.dtype)

        @pl.loop(1, n)
        def _(d):
            regroup(b, lax.rem(b + d, n), c).start()

        pltpu.make_async_copy(
            f_v.at[c, pl.ds(pl.multiple_of(b * rows, rows), rows), :],
            g_v.at[:, pl.ds(pl.multiple_of(b * per + c * w, w), w)], x_send.at[b, c],
        ).start()

    @pl.loop(0, n * tiles)
    def _(i):
        d_v[i // tiles, row(lax.rem(i, tiles)), :] = jnp.zeros((tile, q), jnp.float32)

    @pl.loop(0, count - 1)
    def _(c):
        arrive(na - 1, c)
        fit(c)

        @pl.loop(0, n * tiles)
        def _(i):
            j, r = i // tiles, lax.rem(i, tiles)
            d_v[j, row(r), :] += product(j, r, c)

    last = count - 1
    arrive(na - 1, last)
    fit(last)

    quad = half == 4
    mid = p // 2
    near = (chip + 1 - 2 * lax.rem(chip, 2), lax.rem(chip + 2, 4))
    far = 3 - chip

    def turn(h):
        if not quad:
            return lax.rem(chip + h, half)
        return jnp.where(h == 0, far, jnp.where(h == 1, near[0], jnp.where(h == 2, near[1], chip)))

    @pl.loop(0, half)
    def _(h):
        j = 2 * turn(h) + 1 - parity

        @pl.loop(0, tiles)
        def _(r):
            m_v[row(r), pl.ds(pl.multiple_of(j * q, q), q)] = (
                d_v[j, row(r), :] + product(j, r, last)
            ).astype(m_v.dtype)

        first(j).start()

    @pl.loop(0, 0 if quad else half)
    def _(h):
        j = 2 * lax.rem(chip + h, half) + parity

        @pl.loop(0, tiles)
        def _(r):
            d_v[j, row(r), :] += product(j, r, last)

    def part(way):
        return pl.ds(way * mid, mid)

    def cast(slot, way):
        j = 2 * slot + parity
        m_v[part(way), pl.ds(pl.multiple_of(j * q, q), q)] = d_v[j, part(way), :].astype(m_v.dtype)

    def piece(slot, way, place, target):
        j = 2 * slot + parity
        return pltpu.make_async_remote_copy(
            src_ref=m_v.at[part(way), pl.ds(pl.multiple_of(j * q, q), q)],
            dst_ref=two_v.at[place, part(way), :], send_sem=two_send.at[way, place],
            recv_sem=two_recv.at[way, place], device_id=(a, 2 * target + parity), device_id_type=MESH,
        )

    def add_in(slot, place, way):
        j = 2 * slot + parity
        d_v[j, part(way), :] += two_v[place, part(way), :].astype(jnp.float32)

    if quad:
        for h in range(4):
            slot = (far, near[0], near[1], chip)[h]

            @pl.loop(0, tiles)
            def _(r, slot=slot):
                d_v[2 * slot + parity, row(r), :] += product(2 * slot + parity, r, last)

            first(2 * slot + parity).wait_recv()

            @pl.loop(0, tiles)
            def _(r, slot=slot):
                j = 2 * slot + parity
                d_v[j, row(r), :] += one_v[slot, row(r), :].astype(jnp.float32)

            if h == 0:
                for way in range(2):
                    cast(far, way)
                    piece(far, way, 0, near[way]).start()
            elif h < 3:
                cast(near[h - 1], h - 1)
                piece(near[h - 1], h - 1, 1, near[h - 1]).start()
    else:
        @pl.loop(1, half)
        def _(h):
            slot = lax.rem(chip + h, half)
            j = 2 * slot + parity
            first(j).wait_recv()

            @pl.loop(0, tiles)
            def _(r):
                m_v[row(r), pl.ds(pl.multiple_of(j * q, q), q)] = (
                    d_v[j, row(r), :] + one_v[slot, row(r), :].astype(jnp.float32)
                ).astype(m_v.dtype)

            second(chip, j).start()

        first(b).wait_recv()

        @pl.loop(0, tiles)
        def _(r):
            d_v[b, row(r), :] += one_v[chip, row(r), :].astype(jnp.float32)

    if quad:
        for way in range(2):
            other = near[1 - way]
            piece(other, way, 0, near[way]).wait_recv()
            add_in(other, 0, way)
            cast(other, way)
            piece(other, way, 2, other).start()

    @pl.loop(0, count)
    def _(c):
        pltpu.make_async_copy(
            f_v.at[c, pl.ds(pl.multiple_of(b * rows, rows), rows), :],
            g_v.at[:, pl.ds(pl.multiple_of(b * per + c * w, w), w)], x_send.at[b, c],
        ).wait()

        @pl.loop(1, n)
        def _(d):
            regroup(lax.rem(b + n - d, n), b, c).wait_recv()

    occ = n * per // virt

    def out_copy(i, slot):
        return pltpu.make_async_copy(
            o_v.at[slot], fitted_ao.at[:, pl.ds(pl.multiple_of(i * ao, ao), ao)], o_sem.at[slot]
        )

    @pl.loop(0, occ)
    def _(i):
        slot = lax.rem(i, 2)

        @pl.when(i >= 2)
        def _():
            out_copy(i - 2, slot).wait()

        o_v[slot] = jnp.dot(
            g_v[:, pl.ds(pl.multiple_of(i * virt, virt), virt)], c_v[...], preferred_element_type=jnp.float32
        ).astype(o_v.dtype)
        out_copy(i, slot).start()

    for i in range(max(occ - 2, 0), occ):
        out_copy(i, i % 2).wait()

    if quad:
        for way in range(2):
            piece(chip, way, 1, near[way]).wait_recv()
            add_in(chip, 1, way)
        for way in range(2):
            piece(chip, way, 2, near[1 - way]).wait_recv()
            add_in(chip, 2, way)
    else:
        @pl.loop(1, half)
        def _(h):
            source = lax.rem(chip + half - h, half)
            second(source, b).wait_recv()

            @pl.loop(0, tiles)
            def _(r):
                d_v[b, row(r), :] += two_v[source, row(r), :].astype(jnp.float32)

    result = pltpu.make_async_copy(d_v.at[b], density, local_sem.at[0])
    result.start()

    @pl.loop(0, half)
    def _(h):
        first(2 * h + 1 - parity).wait_send()

    if quad:
        for way in range(2):
            piece(far, way, 0, near[way]).wait_send()
            piece(near[way], way, 1, near[way]).wait_send()
            piece(near[1 - way], way, 2, near[1 - way]).wait_send()
    else:
        @pl.loop(1, half)
        def _(h):
            second(chip, 2 * lax.rem(chip + h, half) + parity).wait_send()

    @pl.loop(0, count)
    def _(c):
        @pl.loop(1, n)
        def _(d):
            regroup(b, lax.rem(b + d, n), c).wait_send()

        @pl.loop(0, na)
        def _(s):
            @pl.when(jnp.logical_and(s >= a, a > 0))
            def _():
                hop(block_of(s, c), s, c, 0, jnp.maximum(a - 1, 0)).wait_send()

            @pl.when(jnp.logical_and(s <= a, a < na - 1))
            def _():
                hop(block_of(s, c), s, c, 1, jnp.minimum(a + 1, na - 1)).wait_send()

    result.wait()


def shards(na, n, metric, amplitudes, virt_coef):
    p, q = metric.shape
    per = amplitudes.shape[1]
    virt, ao = virt_coef.shape
    count = next(c for c in (8, 4, 2, 1) if per % (128 * c) == 0)
    w = per // count
    rows = p // n
    bf16 = jnp.bfloat16
    dma = pltpu.SemaphoreType.DMA
    return pl.pallas_call(
        functools.partial(kernel, na, n, count),
        out_shape=(
            jax.ShapeDtypeStruct((p, q), jnp.float32),
            jax.ShapeDtypeStruct((rows, n * per // virt * ao), bf16),
        ),
        in_specs=[pl.BlockSpec(memory_space=pl.ANY)] * 3,
        out_specs=(pl.BlockSpec(memory_space=pl.ANY), pl.BlockSpec(memory_space=pl.ANY)),
        scratch_shapes=[
            pltpu.VMEM((p, n * q), bf16),
            pltpu.VMEM((count, na * p, w), bf16),
            pltpu.VMEM((n, p, q), jnp.float32),
            pltpu.VMEM((count, p, w), bf16),
            pltpu.VMEM((rows, n * per), bf16),
            pltpu.VMEM((virt, ao), bf16),
            pltpu.VMEM((n // 2, p, q), bf16),
            pltpu.VMEM((n // 2, p, q), bf16),
            pltpu.VMEM((2, rows, ao), bf16),
            dma((n,)), dma((n,)),
            dma((2, na, count)), dma((na, count)),
            dma((n, count)), dma((n, count)),
            dma((n // 2,)), dma((n // 2,)),
            dma((2, n // 2)), dma((2, n // 2)),
            dma((2,)), dma((count + 2,)),
        ],
        compiler_params=pltpu.CompilerParams(
            collective_id=0, has_side_effects=True, vmem_limit_bytes=67043328
        ),
    )(metric, amplitudes, virt_coef)


def solution(mesh):
    in_specs = (P("aux", "pair"), P("aux", "pair"), P())
    out_specs = (P("aux", "pair"), P(("aux", "pair"), None))
    body = functools.partial(shards, mesh.shape["aux"], mesh.shape["pair"])
    return jax.shard_map(body, mesh=mesh, in_specs=in_specs, out_specs=out_specs, check_vma=False)
```
